32 devices in a mesh: slab: 8 (over z, y), col: 4 (over x, core).
Axes of the slice: x: 2, y: 2, z: 4, core: 2. Of those that a mesh axis runs over, the one named last changes fastest.
Arguments:
- classes: int32 [64, 512], P(('slab', 'col')), may hold values from 0 to 15
- across_coeff: float32 [16], replicated, may hold values from 0.5 to 5
- along_coeff: float32 [16], replicated, may hold values from 0.05 to 0.5
Outputs:
- piece_maps: float32 [32768, 1024], P(('slab', 'col'))
- root_map: float32 [1024, 1024], P(('slab', 'col'))
The draws below stay inside these ranges and needn't reach their ends.
All inputs are finite; a program needn't handle non-finite values.
Results may differ from the reference program's by a relative error of at most 0.0003.
Values sent between devices are 32-bit elements; how exact they have to be, the bound alone decides.
A program may use at most 128 MiB of HBM per device.

```python
import math
from functools import partial
import jax
import jax.numpy as jnp
from jax import lax

E = 512
C = 2
CLASSES = 16
PIECES = 32
COLS = 64


def plant(array, rng, low, high):
    spot = [jax.random.randint(jax.random.fold_in(rng, axis), (), 0, length) for axis, length in enumerate(array.shape)]
    widest = array.shape.index(max(array.shape))
    neighbour = spot[:widest] + [(spot[widest] + 1) % array.shape[widest]] + spot[widest + 1:]
    return array.at[tuple(spot)].set(low).at[tuple(neighbour)].set(high)


def setup_inputs(seed: int = 0) -> dict:
    key_of = jax.random.split(jax.random.key(seed), 4)
    classes = plant(jax.random.randint(key_of[0], (COLS, E), 0, CLASSES), jax.random.fold_in(key_of[0], 1), 0, CLASSES - 1).astype(jnp.int32)
    across_coeff = jnp.clip(jnp.exp(jax.random.uniform(key_of[1], (CLASSES,), jnp.float32, math.log(0.5), math.log(5.0))), 0.5, 5.0)
    along_coeff = jnp.clip(jnp.exp(jax.random.uniform(key_of[2], (CLASSES,), jnp.float32, math.log(0.05), math.log(0.5))), 0.05, 0.5)
    return {"classes": classes, "across_coeff": across_coeff, "along_coeff": along_coeff}


def lookup(classes, values_table):
    levels = jnp.arange(values_table.shape[0], dtype=jnp.int32)
    matches = classes[:, None, :] == levels[None, :, None]
    return jnp.sum(jnp.where(matches, values_table[None, :, None], 0.0), axis=1)

def strip_map(along_col, across_col):
    half_size = along_col.shape[0]
    row_index = lax.broadcasted_iota(jnp.int32, (half_size, half_size), 0)
    col_index = lax.broadcasted_iota(jnp.int32, (half_size, half_size), 1)
    shifted = jnp.roll(along_col, 1)
    vertical = jnp.where(row_index == col_index, (along_col + shifted)[None, :], 0.0)
    vertical = vertical - jnp.where(col_index == (row_index + 1) % half_size, along_col[:, None], 0.0)
    vertical = vertical - jnp.where(row_index == (col_index + 1) % half_size, along_col[None, :], 0.0)
    across_diag = jnp.where(row_index == col_index, across_col[None, :], 0.0)
    upper_rows = jnp.concatenate([vertical + across_diag, -across_diag], axis=1)
    lower_rows = jnp.concatenate([-across_diag, across_diag], axis=1)
    return jnp.concatenate([upper_rows, lower_rows], axis=0)

def quarters(full_map):
    half_size = full_map.shape[0] // 2
    return (full_map[:half_size, :half_size], full_map[:half_size, half_size:], full_map[half_size:, :half_size], full_map[half_size:, half_size:])

def merge_blocks(left_upper, left_lower_left, left_lower, right_upper, right_upper_right, right_lower):
    half_size = left_upper.shape[0]
    factor = jnp.linalg.cholesky(left_lower + right_upper)
    coupled = jnp.concatenate([left_lower_left, right_upper_right], axis=1)
    scaled = lax.linalg.triangular_solve(factor, coupled, left_side=True, lower=True)
    product = lax.dot_general(scaled, scaled, (((0,), (0,)), ((), ())), precision=lax.Precision.HIGHEST)
    zero_block = jnp.zeros((half_size, half_size), left_upper.dtype)
    diagonal_part = jnp.concatenate([jnp.concatenate([left_upper, zero_block], axis=1), jnp.concatenate([zero_block, right_lower], axis=1)], axis=0)
    return diagonal_part - product

def merge_maps(left_map, right_map):
    left_upper, left_upper_right, left_lower_left, left_lower = quarters(left_map)
    right_upper, right_upper_right, right_lower_left, right_lower = quarters(right_map)
    return merge_blocks(left_upper, left_lower_left, left_lower, right_upper, right_upper_right, right_lower)

def build_piece(piece_classes, across_coeff, along_coeff):
    across = lookup(piece_classes, across_coeff)
    along = lookup(piece_classes, along_coeff)
    own_map = strip_map(along[0], across[0])
    for column in range(1, piece_classes.shape[0]):
        own_map = merge_maps(own_map, strip_map(along[column], across[column]))
    return own_map

def advance(running, own_map):
    return (merge_maps(running, own_map), None)

def reference(classes, across_coeff, along_coeff):
    grouped = classes.reshape(PIECES, C, E)
    pieces = lax.map(partial(build_piece, across_coeff=across_coeff, along_coeff=along_coeff), grouped)
    root_map, unused = lax.scan(advance, pieces[0], pieces[1:])
    return (pieces.reshape(PIECES * 2 * E, 2 * E), root_map)
```

```python
import functools
import jax
import jax.numpy as jnp
from jax import lax
from jax.experimental import pallas as pl
from jax.experimental.pallas import tpu as pltpu
from jax.sharding import PartitionSpec as P

PRODUCT = lax.Precision.HIGH
AXES = ("slab", "col")


def swapped(block, axis, stride):
    count = lax.axis_size(axis)
    route = []
    for low in range(count):
        high = low | 1 << stride
        if high != low and high < count:
            route += [(low, high), (high, low)]
    return lax.ppermute(block, axis, route)


def lookup(classes, values_table):
    levels = jnp.arange(values_table.shape[0], dtype=jnp.int32)
    matches = classes[:, None, :] == levels[None, :, None]
    return jnp.sum(jnp.where(matches, values_table[None, :, None], 0.0), axis=1)


def strip_map(along_col, across_col):
    half_size = along_col.shape[0]
    row_index = lax.broadcasted_iota(jnp.int32, (half_size, half_size), 0)
    col_index = lax.broadcasted_iota(jnp.int32, (half_size, half_size), 1)
    shifted = jnp.roll(along_col, 1)
    vertical = jnp.where(row_index == col_index, (along_col + shifted)[None, :], 0.0)
    vertical = vertical - jnp.where(
        col_index == (row_index + 1) % half_size, along_col[:, None], 0.0
    )
    vertical = vertical - jnp.where(
        row_index == (col_index + 1) % half_size, along_col[None, :], 0.0
    )
    across_diag = jnp.where(row_index == col_index, across_col[None, :], 0.0)
    upper_rows = jnp.concatenate([vertical + across_diag, -across_diag], axis=1)
    lower_rows = jnp.concatenate([-across_diag, across_diag], axis=1)
    return jnp.concatenate([upper_rows, lower_rows], axis=0)


def quarters(full_map):
    half_size = full_map.shape[0] // 2
    return (
        full_map[:half_size, :half_size],
        full_map[:half_size, half_size:],
        full_map[half_size:, :half_size],
        full_map[half_size:, half_size:],
    )


def blocked_factor(matrix):
    size_total = matrix.shape[0]
    panel = 128
    columns = []
    remaining = matrix
    for start in range(0, size_total, panel):
        head = remaining[:panel, :panel]
        head_factor = jnp.linalg.cholesky(head)
        if remaining.shape[0] > panel:
            below = remaining[panel:, :panel]
            below_factor = lax.linalg.triangular_solve(
                head_factor, below, left_side=False, lower=True, transpose_a=True
            )
            remaining = remaining[panel:, panel:] - lax.dot_general(
                below_factor,
                below_factor,
                (((1,), (1,)), ((), ())),
                precision=lax.Precision.HIGHEST,
            )
            block_column = jnp.concatenate([head_factor, below_factor], axis=0)
        else:
            block_column = head_factor
        if start > 0:
            block_column = jnp.concatenate(
                [jnp.zeros((start, panel), matrix.dtype), block_column], axis=0
            )
        columns.append(block_column)
    return jnp.concatenate(columns, axis=1)


def merge_blocks(
    left_upper, left_lower_left, left_lower, right_upper, right_upper_right, right_lower
):
    half_size = left_upper.shape[0]
    factor = blocked_factor(left_lower + right_upper)
    coupled = jnp.concatenate([left_lower_left, right_upper_right], axis=1)
    scaled = lax.linalg.triangular_solve(factor, coupled, left_side=True, lower=True)
    product = lax.dot_general(
        scaled, scaled, (((0,), (0,)), ((), ())), precision=lax.Precision.HIGHEST
    )
    zero_block = jnp.zeros((half_size, half_size), left_upper.dtype)
    diagonal_part = jnp.concatenate(
        [
            jnp.concatenate([left_upper, zero_block], axis=1),
            jnp.concatenate([zero_block, right_lower], axis=1),
        ],
        axis=0,
    )
    return diagonal_part - product


def merge_maps(left_map, right_map):
    left_upper, left_upper_right, left_lower_left, left_lower = quarters(left_map)
    right_upper, right_upper_right, right_lower_left, right_lower = quarters(right_map)
    return merge_blocks(
        left_upper, left_lower_left, left_lower, right_upper, right_upper_right, right_lower
    )


def level_payload(merged, is_right):
    upper, upper_right, lower_left, lower = quarters(merged)
    middle = jnp.where(is_right, upper_right, lower_left)
    payload = jnp.stack([upper, middle, lower])
    return payload


def joined(merged, received, is_right):
    upper, upper_right, lower_left, lower = quarters(merged)
    partner_upper = received[0]
    partner_middle = received[1]
    partner_lower = received[2]
    left_upper = jnp.where(is_right, partner_upper, upper)
    left_lower_left = jnp.where(is_right, partner_middle, lower_left)
    left_lower = jnp.where(is_right, partner_lower, lower)
    right_upper = jnp.where(is_right, upper, partner_upper)
    right_upper_right = jnp.where(is_right, upper_right, partner_middle)
    right_lower = jnp.where(is_right, lower, partner_lower)
    return merge_blocks(
        left_upper, left_lower_left, left_lower, right_upper, right_upper_right, right_lower
    )


def local_columns(classes, across_coeff, along_coeff):
    across = lookup(classes, across_coeff)
    along = lookup(classes, along_coeff)
    own_map = piece_map(across, along)
    col_levels = lax.axis_size("col").bit_length() - 1
    slab_levels = lax.axis_size("slab").bit_length() - 1
    merged = own_map
    for height in range(col_levels):
        is_right = lax.axis_index("col") >> height & 1 == 1
        received = swapped(level_payload(merged, is_right), "col", height)
        merged = joined(merged, received, is_right)
    for height in range(slab_levels):
        is_right = lax.axis_index("slab") >> height & 1 == 1
        received = swapped(level_payload(merged, is_right), "slab", height)
        merged = joined(merged, received, is_right)
    share_rows = merged.shape[0] // lax.axis_size(("slab", "col"))
    root_rows = lax.dynamic_slice_in_dim(
        merged, lax.axis_index(("slab", "col")) * share_rows, share_rows, 0
    )
    return (own_map, root_rows)


def piece_kernel(size, rows, vec_ref, cols_ref, o_ref, coef):
    levels = size.bit_length() - 1
    i = pl.program_id(0)

    def back(x, s):
        return pltpu.roll(x, s, 1)

    def fore(x, s):
        return pltpu.roll(x, size - s, 1)

    @pl.when(i == 0)
    def _():
        def wide(k):
            return jnp.broadcast_to(vec_ref[k : k + 1, :], (8, size))

        a0, a1, al0, al1 = wide(0), wide(1), wide(2), wide(3)
        sh1 = back(al1, 1)
        diag = a0 + a1 + al1 + sh1
        inv = 1.0 / diag
        coef[0] = inv
        lo = -sh1 * inv
        hi = -al1 * inv
        for level in range(levels - 1):
            s = 1 << level
            fix = 1.0 / (1.0 - lo * back(hi, s) - hi * fore(lo, s))
            coef[3 * level + 1] = -lo
            coef[3 * level + 2] = -hi
            coef[3 * level + 3] = fix
            lo, hi = -lo * back(lo, s) * fix, -hi * fore(hi, s) * fix
        g = lo + hi
        h = back(g, size // 2)
        coef[3 * levels - 2] = -g
        coef[3 * levels - 1] = 1.0 / (1.0 - g * h)

    def co(k):
        return coef[k, 0:1, :]

    row = lax.broadcasted_iota(jnp.int32, (rows, size), 0) + i * rows
    col = lax.broadcasted_iota(jnp.int32, (rows, size), 1)
    x = jnp.where(row == col, co(0), 0.0)
    for level in range(levels - 1):
        s = 1 << level
        x = (x + co(3 * level + 1) * back(x, s) + co(3 * level + 2) * fore(x, s)) * co(3 * level + 3)
    x = (x + co(3 * levels - 2) * back(x, size // 2)) * co(3 * levels - 1)
    a0, a1, al0 = vec_ref[0:1, :], vec_ref[1:2, :], vec_ref[2:3, :]
    sh0 = jnp.broadcast_to(vec_ref[4:5, :], (1, size))
    r0, r1 = cols_ref[:, 0:1], cols_ref[:, 1:2]
    vert = jnp.where(row == col, al0 + sh0 + a0, 0.0)
    vert = vert - jnp.where(row == jnp.where(col == size - 1, 0, col + 1), al0, 0.0)
    vert = vert - jnp.where(col == jnp.where(row == size - 1, 0, row + 1), sh0, 0.0)
    x0, x1 = x * a0, x * a1
    o_ref[0, :, :size] = vert - r0 * x0
    o_ref[0, :, size:] = -(r0 * x1)
    o_ref[1, :, :size] = -(r1 * x0)
    o_ref[1, :, size:] = jnp.where(row == col, a1, 0.0) - r1 * x1


def piece_map(across, along):
    size = across.shape[1]
    rows = 32
    vecs = jnp.concatenate([across, along, jnp.roll(along, 1, axis=1), along], axis=0)
    out = pl.pallas_call(
        functools.partial(piece_kernel, size, rows),
        grid=(size // rows,),
        out_shape=jax.ShapeDtypeStruct((2, size, 2 * size), jnp.float32),
        in_specs=[
            pl.BlockSpec((8, size), lambda i: (0, 0)),
            pl.BlockSpec((rows, 2), lambda i: (i, 0)),
        ],
        out_specs=pl.BlockSpec((2, rows, 2 * size), lambda i: (0, i, 0)),
        scratch_shapes=[pltpu.VMEM((3 * (size.bit_length() - 1), 8, size), jnp.float32)],
    )(vecs, across.T)
    return out.reshape(2 * size, 2 * size)


def gather_kernel(slabs, cols, x_ref, o_ref, send, recv, pass_send, pass_recv, own):
    half = cols // 2
    pairs = slabs * half
    slab, col = lax.axis_index("slab"), lax.axis_index("col")
    pair, odd = slab * half + col // 2, lax.rem(col, 2)
    me = slab * cols + col

    def place(q, side):
        return {"slab": q // half, "col": lax.rem(q, half) * 2 + side}

    def index(q, side):
        return q * 2 + side

    def to(step):
        return lax.rem(pair + step, pairs)

    def copy(src, at, sems, step, device):
        return pltpu.make_async_remote_copy(
            src_ref=src,
            dst_ref=o_ref.at[at],
            send_sem=sems[0].at[step],
            recv_sem=sems[1].at[step],
            device_id=device,
            device_id_type=pl.DeviceIdType.MESH,
        )

    barrier = pltpu.get_barrier_semaphore()
    sibling = place(pair, 1 - odd)
    for step in range(1, pairs):
        pl.semaphore_signal(
            barrier, inc=1, device_id=place(to(step), odd), device_id_type=pl.DeviceIdType.MESH
        )
    pl.semaphore_signal(barrier, inc=1, device_id=sibling, device_id_type=pl.DeviceIdType.MESH)
    pl.semaphore_wait(barrier, pairs)

    local_copy = pltpu.make_async_copy(x_ref, o_ref.at[me], own)
    local_copy.start()
    out = [copy(x_ref, me, (send, recv), step, place(to(step), odd)) for step in range(1, pairs)]
    for c in out:
        c.start()
    passed = [copy(x_ref, me, (pass_send, pass_recv), 0, sibling)]
    passed[0].start()
    for step in range(1, pairs):
        at = index(to(pairs - step), odd)
        copy(x_ref, at, (send, recv), step, sibling).wait_recv()
        c = copy(o_ref.at[at], at, (pass_send, pass_recv), step, sibling)
        c.start()
        passed.append(c)
    for step in range(pairs):
        at = index(to(pairs - step), 1 - odd)
        copy(x_ref, at, (pass_send, pass_recv), step, sibling).wait_recv()
    for c in out + passed:
        c.wait_send()
    local_copy.wait()


def gathered(block, number):
    slabs, cols = lax.axis_size("slab"), lax.axis_size("col")
    if cols % 2:
        return lax.all_gather(block, AXES, axis=0)
    pairs = slabs * cols // 2
    return pl.pallas_call(
        functools.partial(gather_kernel, slabs, cols),
        out_shape=jax.ShapeDtypeStruct((slabs * cols,) + block.shape, block.dtype),
        in_specs=[pl.BlockSpec(memory_space=pltpu.VMEM)],
        out_specs=pl.BlockSpec(memory_space=pltpu.VMEM),
        scratch_shapes=[pltpu.SemaphoreType.DMA((pairs,))] * 4 + [pltpu.SemaphoreType.DMA],
        compiler_params=pltpu.CompilerParams(collective_id=number, has_side_effects=True),
    )(block)


LANES = 128
SUBS = 8


def spread(x):
    return jnp.broadcast_to(x, (SUBS, LANES))


def tree(terms):
    while len(terms) > 1:
        terms = [sum(terms[k : k + 2][1:], terms[k]) for k in range(0, len(terms), 2)]
    return terms[0]


def small_inverse(v):
    size = len(v)
    v = [list(row) for row in v]
    for k in range(0, size, 2):
        p, q, r = v[k][k], v[k][k + 1], v[k + 1][k + 1]
        inv = 1.0 / (p * r - q * q)
        others = [i for i in range(size) if i not in (k, k + 1)]
        c = {i: (v[min(i, k)][max(i, k)], v[min(i, k + 1)][max(i, k + 1)]) for i in others}
        s = {}
        for i in others:
            x, y = c[i]
            s[i] = ((r * x - q * y) * inv, (p * y - q * x) * inv)
        for i in others:
            for j in others:
                if i <= j:
                    v[i][j] = v[i][j] - (s[i][0] * c[j][0] + s[i][1] * c[j][1])
        for i in others:
            sign = 1.0 if i < k else -1.0
            for d in range(2):
                v[min(i, k + d)][max(i, k + d)] = s[i][d]
        v[k][k], v[k][k + 1], v[k + 1][k + 1] = -(r * inv), q * inv, -(p * inv)
    return [[-v[min(i, j)][max(i, j)] for j in range(size)] for i in range(size)]


def eliminate(g, n, vals, invs):
    count = len(g)
    for p in range(n // SUBS):
        at = p * SUBS
        for j in range(SUBS):
            for b in range(count):
                vals[j, b * SUBS : (b + 1) * SUBS] = spread(g[b][p][0][:, at + j : at + j + 1])
        v = [
            [vals[j, pl.ds(i, SUBS, stride=SUBS)] if i <= j else None for j in range(SUBS)]
            for i in range(SUBS)
        ]
        w = small_inverse(v)
        for j in range(SUBS):
            for i in range(SUBS):
                invs[j, i * SUBS : (i + 1) * SUBS] = w[i][j]
        for b in range(count):
            m = [invs[j, pl.ds(b, SUBS, stride=SUBS)] for j in range(SUBS)]
            s = [
                tree([m[j] * spread(half[j : j + 1]) for j in range(SUBS)]) for half in g[b][p]
            ]
            rows = [i for i in range(n // SUBS) if i != p]
            old = {i: g[b][i][0] for i in rows}
            for j in range(SUBS):
                wide = [spread(half[j : j + 1]) for half in s]
                for i in rows:
                    c = spread(old[i][:, at + j : at + j + 1])
                    g[b][i] = [half - c * wide[h] for h, half in enumerate(g[b][i])]
            g[b][p] = s
    return g


def halves(x):
    return [x[:, :LANES], x[:, LANES:]]


def parts(x):
    high = x.astype(jnp.bfloat16)
    return high, (x - high.astype(jnp.float32)).astype(jnp.bfloat16)


def contract(a, b, dim):
    def dot(x, y):
        return lax.dot_general(
            x, y, (((dim,), (0,)), ((), ())), preferred_element_type=jnp.float32
        )

    (ah, al), (bh, bl) = parts(a), parts(b)
    return dot(ah, bh) + (dot(ah, bl) + dot(al, bh))


def product(a, b):
    return contract(a, b, 1)


def product_t(a, b):
    return contract(a, b, 0)


def merge_group(src, dst, keep, lefts, n, vals, invs):
    rows = src.shape[1]
    g = [
        [
            halves(src[2 * l, n + k : n + k + SUBS] + src[2 * l + 1, k : k + SUBS])
            for k in range(0, n, SUBS)
        ]
        for l in lefts
    ]
    g = eliminate(g, n, vals, invs)
    lane = lax.broadcasted_iota(jnp.int32, (1, LANES), 1)
    for l, x in zip(lefts, g):
        z = jnp.concatenate([jnp.concatenate(h, axis=1) for h in x], axis=0)
        if keep is not None:
            keep[l] = z
        top, low = src[2 * l, 0:n], src[2 * l + 1, n : 2 * n]
        base = [top, low]
        if rows > 2 * n:
            base.append(src[2 * l, 2 * n :] + src[2 * l + 1, 2 * n :])
        base = jnp.concatenate(base, axis=0)
        new = base - product(base[:, :n], z)
        v0, v1 = halves(new)
        if dst is None:
            return v0, v1
        odd = l % 2
        if isinstance(odd, int):
            if odd:
                v0, v1 = jnp.where(lane < n, pltpu.roll(v0, n, 1), 0.0), v1
            else:
                v0, v1 = jnp.where(lane < n, v1, v0), jnp.where(lane < n, 0.0, v1)
        dst[l, :, :LANES] = v0
        dst[l, :, LANES:] = v1


def local_kernel(n, height, cls_ref, ac_ref, al_ref, o_ref, first, second, vals, invs):
    k = 2 * height
    lane = lax.broadcasted_iota(jnp.int32, (1, LANES), 1)
    cls = cls_ref[...]
    across = jnp.zeros(cls.shape, jnp.float32)
    along = jnp.zeros(cls.shape, jnp.float32)
    for level in range(ac_ref.shape[0]):
        across = jnp.where(cls == level, ac_ref[level], across)
        along = jnp.where(cls == level, al_ref[level], along)
    inner = (lane > 0) & (lane < n)
    link = jnp.where(inner, along, 0.0)
    before = pltpu.roll(across, 1, 1)
    off = jnp.where(inner, across, 0.0)
    i = lax.broadcasted_iota(jnp.int32, (n, LANES), 0)
    j = lax.broadcasted_iota(jnp.int32, (n, LANES), 1)
    kr = lax.broadcasted_iota(jnp.int32, (k, LANES), 0)
    kl = lax.broadcasted_iota(jnp.int32, (k, LANES), 1)
    zero = jnp.zeros((n, LANES), jnp.float32)
    for h in range(height):
        a, prev = across[h + 1 : h + 2], link[h : h + 1]
        diag = jnp.where(inner, before[h + 1 : h + 2] + a + along[h : h + 1] + along[h + 1 : h + 2], 1.0)
        right = off[h + 1 : h + 2]
        left = jnp.where(lane > 0, pltpu.roll(right, 1, 1), 0.0)
        bb = jnp.where(i == j, diag, 0.0) - jnp.where(j == i + 1, left, 0.0) - jnp.where(i == j + 1, right, 0.0)
        bb = jnp.where(j < n, bb, 0.0)
        tb = -jnp.where((i == j) & (j < n), prev, 0.0)
        a0, a1 = a[:, 0:1], a[:, n - 1 : n]
        fb = -jnp.where((i == 1) & (j == n + h), a0, 0.0) - jnp.where((i == n - 1) & (j == n + height + h), a1, 0.0)
        ft = -jnp.where((kr == h) & (kl == 1), a0, 0.0) - jnp.where((kr == height + h) & (kl == n - 1), a1, 0.0)
        if h % 2:
            first[h, 0:n, :LANES] = zero
            first[h, 0:n, LANES:] = tb
            first[h, n : 2 * n, :LANES] = tb
            first[h, n : 2 * n, LANES:] = bb + fb
            first[h, 2 * n :, :LANES] = jnp.zeros((k, LANES), jnp.float32)
            first[h, 2 * n :, LANES:] = ft
        else:
            first[h, 0:n, :LANES] = tb
            first[h, 0:n, LANES:] = zero
            first[h, n : 2 * n, :LANES] = bb + pltpu.roll(tb, n, 1)
            first[h, n : 2 * n, LANES:] = fb
            first[h, 2 * n :, :LANES] = ft
            first[h, 2 * n :, LANES:] = jnp.zeros((k, LANES), jnp.float32)
    count, src, dst = height // 2, first, second
    while count > 1:
        merge_group(src, dst, None, list(range(count)), n, vals, invs)
        src, dst, count = dst, src, count // 2
    v0, v1 = merge_group(src, None, None, [0], n, vals, invs)
    top = jnp.where(lane < n, pltpu.roll(v0[:n], n, 1), pltpu.roll(v1[:n], n, 1))
    o_ref[0:n] = top
    o_ref[n : 2 * n] = jnp.where(lane < n + k, v1[n : 2 * n], pltpu.roll(v1[:n], k, 1))
    kk = v1[2 * n :]
    packed = None
    for q in range(k // SUBS):
        piece = pltpu.roll(kk[q * SUBS : (q + 1) * SUBS], (q * k - n) % LANES, 1)
        packed = piece if q == 0 else jnp.where(lane // k == q, piece, packed)
    o_ref[2 * n :] = packed


def local_strip(cls, across_coeff, along_coeff, n, height):
    k = 2 * height
    rows = 2 * n + k
    return pl.pallas_call(
        functools.partial(local_kernel, n, height),
        out_shape=jax.ShapeDtypeStruct((2 * n + SUBS, LANES), jnp.float32),
        in_specs=[
            pl.BlockSpec(memory_space=pltpu.VMEM),
            pl.BlockSpec(memory_space=pltpu.SMEM),
            pl.BlockSpec(memory_space=pltpu.SMEM),
        ],
        out_specs=pl.BlockSpec(memory_space=pltpu.VMEM),
        scratch_shapes=[
            pltpu.VMEM((height, rows, 2 * LANES), jnp.float32),
            pltpu.VMEM((height // 2, rows, 2 * LANES), jnp.float32),
            pltpu.VMEM((SUBS, SUBS * SUBS, LANES), jnp.float32),
            pltpu.VMEM((SUBS, SUBS * SUBS, LANES), jnp.float32),
        ],
    )(cls, across_coeff, along_coeff)


def ring_kernel(n, height, where_ref, x_ref, o_ref, first, second, kept, xs, vals, invs):
    strips = x_ref.shape[0]
    k = 2 * height
    lane = lax.broadcasted_iota(jnp.int32, (1, LANES), 1)
    s0, side = where_ref[0], where_ref[1]
    left_half = lane < n

    @pl.loop(0, strips // 2)
    def _(q):
        a0, a1 = x_ref[2 * q, 0:n], x_ref[2 * q, n : 2 * n]
        b0, b1 = x_ref[2 * q + 1, 0:n], x_ref[2 * q + 1, n : 2 * n]
        both = jnp.where(left_half, pltpu.roll(a0, n, 1), b0)
        both = jnp.concatenate([both, jnp.zeros((n, LANES), jnp.float32)], axis=0).T
        zero = jnp.zeros((n, LANES), jnp.float32)
        e, f = 2 * q, 2 * q + 1
        first[e, 0:n, :LANES] = pltpu.roll(a0, n, 1)
        first[e, 0:n, LANES:] = zero
        first[e, n : 2 * n, :LANES] = jnp.where(left_half, a1, pltpu.roll(both[:n], n, 1))
        first[e, n : 2 * n, LANES:] = zero
        first[f, 0:n, :LANES] = jnp.where(left_half, b0, 0.0)
        first[f, 0:n, LANES:] = jnp.where(left_half, pltpu.roll(b0, n, 1), 0.0)
        first[f, n : 2 * n, :LANES] = both[n:]
        first[f, n : 2 * n, LANES:] = jnp.where(left_half, b1, 0.0)

    for a in range(2):
        s = s0 + a
        low = x_ref[s, n : 2 * n]
        mine = (lane >= n + a * height) & (lane < n + (a + 1) * height)
        shift = (a - side) * height
        fb = jnp.where(mine, pltpu.roll(low, lax.rem(shift + LANES, LANES), 1), 0.0)
        ft = jnp.where(mine, pltpu.roll(low, lax.rem(shift - k + LANES, LANES), 1), 0.0)
        first[s, 0:n, LANES:] += ft
        first[s, n : 2 * n, LANES:] += fb

    count, src, dst, base = strips // 2, first, second, 0
    bases = []
    while count > 1:
        keep = kept.at[pl.ds(base, count)]
        if count > SUBS:
            @pl.loop(0, count // SUBS)
            def _(g):
                at = g * SUBS
                merge_group(
                    src.at[pl.ds(2 * at, 2 * SUBS)], dst.at[pl.ds(at, SUBS)],
                    keep.at[pl.ds(at, SUBS)], list(range(SUBS)), n, vals, invs,
                )
        else:
            merge_group(src, dst, keep, list(range(count)), n, vals, invs)
        bases.append((base, count))
        base += count
        src, dst, count = dst, src, count // 2
    bases.append((base, 1))
    v0, v1 = merge_group(src, None, kept.at[pl.ds(base, 1)], [0], n, vals, invs)
    t_rows, b_rows = v0[:n], v0[n:]
    d = pltpu.roll(v0[:n], n, 1) + v1[:n] + pltpu.roll(v0[n:], n, 1) + v1[n:]
    f = v1[:n] + v1[n:]
    d = jnp.where(left_half, d, 0.0)
    g = [[[d[r : r + SUBS], f[r : r + SUBS]] for r in range(0, n, SUBS)]]
    g = eliminate(g, n, vals, invs)
    x = jnp.concatenate([h[1] for h in g[0]], axis=0)
    xs[strips - 1] = x
    step = strips // 2
    for base, count in reversed(bases):
        for l in range(count):
            at = (2 * l + 1) * step - 1
            t_at, b_at = (at - step) % strips, (at + step) % strips
            z = kept[base + l]
            both = jnp.concatenate([xs[t_at], xs[b_at]], axis=0)
            zz = jnp.where(left_half, pltpu.roll(z[:, :LANES], n, 1), pltpu.roll(z[:, LANES:], n, 1))
            xs[at] = z[:, LANES:] - product(zz, both)
        step //= 2

    outs = [[None] * (strips * height // LANES) for _ in range(2)]
    per = LANES // height
    for s in range(strips):
        xx = jnp.where(left_half, pltpu.roll(xs[s], n, 1), xs[(s - 1) % strips])
        r = product_t(xx, x_ref[s, n : 2 * n])
        r = r[:k] + pltpu.roll(r[n : n + k], LANES - k, 1)
        block, spot = s // per, s % per
        for side_of in range(2):
            piece = pltpu.roll(r, (spot * height - n - side_of * height) % LANES, 1)
            old = outs[side_of][block]
            outs[side_of][block] = -piece if old is None else jnp.where(lane // height == spot, -piece, old)
    o_ref[...] = jnp.concatenate(outs[0] + outs[1], axis=1)
    for a in range(2):
        s = s0 + a
        kk = x_ref[s, 2 * n : 2 * n + SUBS]
        spot, block = lax.rem(s, per), s // per
        for h in range(height // SUBS):
            q = side * (height // SUBS) + h
            for side_of in range(2):
                shift = spot * height - q * k - side_of * height + 4 * LANES
                piece = pltpu.roll(kk, lax.rem(shift, LANES), 1)
                at = pl.multiple_of((side_of * (strips // per) + block) * LANES, LANES)
                rows = pl.ds(a * height + h * SUBS, SUBS)
                o_ref[rows, pl.ds(at, LANES)] += jnp.where(lane // height == spot, piece, 0.0)


def ring_rows(where, wide, n, height):
    strips, k = wide.shape[0], 2 * height
    return pl.pallas_call(
        functools.partial(ring_kernel, n, height),
        out_shape=jax.ShapeDtypeStruct((k, k * strips), jnp.float32),
        in_specs=[
            pl.BlockSpec(memory_space=pltpu.SMEM),
            pl.BlockSpec(memory_space=pltpu.VMEM),
        ],
        out_specs=pl.BlockSpec(memory_space=pltpu.VMEM),
        scratch_shapes=[
            pltpu.VMEM((strips, 2 * n, 2 * LANES), jnp.float32),
            pltpu.VMEM((strips // 2, 2 * n, 2 * LANES), jnp.float32),
            pltpu.VMEM((strips, n, 2 * LANES), jnp.float32),
            pltpu.VMEM((strips, n, LANES), jnp.float32),
            pltpu.VMEM((SUBS, SUBS * SUBS, LANES), jnp.float32),
            pltpu.VMEM((SUBS, SUBS * SUBS, LANES), jnp.float32),
        ],
    )(where, wide)


def local_rows(classes, across_coeff, along_coeff):
    own_across = lookup(classes, across_coeff)
    own_along = lookup(classes, along_coeff)
    devices = lax.axis_size(AXES)
    me = lax.axis_index(AXES)
    size = classes.shape[1]
    cols = classes.shape[0] * devices
    height = size // devices
    everyone = gathered(classes, 0).reshape(cols, size)
    own_map = piece_map(own_across, own_along)
    padded = jnp.concatenate([everyone[:, size - 1 :], everyone], axis=1)
    mine = lax.dynamic_slice_in_dim(padded, me * height, height + 1, 1).T
    mine = jnp.pad(mine, ((0, -(height + 1) % SUBS), (0, LANES - cols)))
    wide = gathered(local_strip(mine, across_coeff, along_coeff, cols, height), 1)
    share = 2 * size // devices
    start = me * share
    side = start // size
    where = jnp.stack([(start - side * size) // height, side]).astype(jnp.int32)
    rows = ring_rows(where, wide, cols, height)

    first_ac = lookup(everyone[:1], across_coeff)
    last_ac = lookup(everyone[cols - 1 :], across_coeff)
    al = lookup(everyone[:1], along_coeff)
    sh = jnp.roll(al, 1, axis=1)
    zero = jnp.zeros_like(al)
    on = jnp.concatenate([first_ac + al + sh, last_ac], axis=1)
    below = jnp.concatenate([al, zero], axis=1)
    above = jnp.concatenate([sh, zero], axis=1)
    row = lax.broadcasted_iota(jnp.int32, (share, 2 * size), 0) + start
    col = lax.broadcasted_iota(jnp.int32, (share, 2 * size), 1)
    rows = rows + jnp.where(row == col, on, 0.0)
    rows = rows - jnp.where((row == (col + 1) % size) & (row < size) & (col < size), below, 0.0)
    rows = rows - jnp.where((col == (row + 1) % size) & (row < size) & (col < size), above, 0.0)
    return own_map, rows


def local(classes, across_coeff, along_coeff):
    devices = lax.axis_size(AXES)
    cols = classes.shape[0] * devices
    height = classes.shape[1] // devices
    if 2 * cols == LANES and 4 * height == cols:
        return local_rows(classes, across_coeff, along_coeff)
    return local_columns(classes, across_coeff, along_coeff)


def solution(mesh):
    placed = (P(("slab", "col"), None), P(), P())
    return jax.shard_map(
        local,
        mesh=mesh,
        in_specs=placed,
        out_specs=(P(("slab", "col"), None), P(("slab", "col"), None)),
        check_vma=False,
    )
```

```python
import functools
import jax
import jax.numpy as jnp
from jax import lax
from jax.experimental import pallas as pl
from jax.experimental.pallas import tpu as pltpu
from jax.sharding import PartitionSpec as P

PRODUCT = lax.Precision.HIGH
AXES = ("slab", "col")


def swapped(block, axis, stride):
    count = lax.axis_size(axis)
    route = []
    for low in range(count):
        high = low | 1 << stride
        if high != low and high < count:
            route += [(low, high), (high, low)]
    return lax.ppermute(block, axis, route)


def lookup(classes, values_table):
    levels = jnp.arange(values_table.shape[0], dtype=jnp.int32)
    matches = classes[:, None, :] == levels[None, :, None]
    return jnp.sum(jnp.where(matches, values_table[None, :, None], 0.0), axis=1)


def strip_map(along_col, across_col):
    half_size = along_col.shape[0]
    row_index = lax.broadcasted_iota(jnp.int32, (half_size, half_size), 0)
    col_index = lax.broadcasted_iota(jnp.int32, (half_size, half_size), 1)
    shifted = jnp.roll(along_col, 1)
    vertical = jnp.where(row_index == col_index, (along_col + shifted)[None, :], 0.0)
    vertical = vertical - jnp.where(
        col_index == (row_index + 1) % half_size, along_col[:, None], 0.0
    )
    vertical = vertical - jnp.where(
        row_index == (col_index + 1) % half_size, along_col[None, :], 0.0
    )
    across_diag = jnp.where(row_index == col_index, across_col[None, :], 0.0)
    upper_rows = jnp.concatenate([vertical + across_diag, -across_diag], axis=1)
    lower_rows = jnp.concatenate([-across_diag, across_diag], axis=1)
    return jnp.concatenate([upper_rows, lower_rows], axis=0)


def quarters(full_map):
    half_size = full_map.shape[0] // 2
    return (
        full_map[:half_size, :half_size],
        full_map[:half_size, half_size:],
        full_map[half_size:, :half_size],
        full_map[half_size:, half_size:],
    )


def blocked_factor(matrix):
    size_total = matrix.shape[0]
    panel = 128
    columns = []
    remaining = matrix
    for start in range(0, size_total, panel):
        head = remaining[:panel, :panel]
        head_factor = jnp.linalg.cholesky(head)
        if remaining.shape[0] > panel:
            below = remaining[panel:, :panel]
            below_factor = lax.linalg.triangular_solve(
                head_factor, below, left_side=False, lower=True, transpose_a=True
            )
            remaining = remaining[panel:, panel:] - lax.dot_general(
                below_factor,
                below_factor,
                (((1,), (1,)), ((), ())),
                precision=lax.Precision.HIGHEST,
            )
            block_column = jnp.concatenate([head_factor, below_factor], axis=0)
        else:
            block_column = head_factor
        if start > 0:
            block_column = jnp.concatenate(
                [jnp.zeros((start, panel), matrix.dtype), block_column], axis=0
            )
        columns.append(block_column)
    return jnp.concatenate(columns, axis=1)


def merge_blocks(
    left_upper, left_lower_left, left_lower, right_upper, right_upper_right, right_lower
):
    half_size = left_upper.shape[0]
    factor = blocked_factor(left_lower + right_upper)
    coupled = jnp.concatenate([left_lower_left, right_upper_right], axis=1)
    scaled = lax.linalg.triangular_solve(factor, coupled, left_side=True, lower=True)
    product = lax.dot_general(
        scaled, scaled, (((0,), (0,)), ((), ())), precision=lax.Precision.HIGHEST
    )
    zero_block = jnp.zeros((half_size, half_size), left_upper.dtype)
    diagonal_part = jnp.concatenate(
        [
            jnp.concatenate([left_upper, zero_block], axis=1),
            jnp.concatenate([zero_block, right_lower], axis=1),
        ],
        axis=0,
    )
    return diagonal_part - product


def merge_maps(left_map, right_map):
    left_upper, left_upper_right, left_lower_left, left_lower = quarters(left_map)
    right_upper, right_upper_right, right_lower_left, right_lower = quarters(right_map)
    return merge_blocks(
        left_upper, left_lower_left, left_lower, right_upper, right_upper_right, right_lower
    )


def level_payload(merged, is_right):
    upper, upper_right, lower_left, lower = quarters(merged)
    middle = jnp.where(is_right, upper_right, lower_left)
    payload = jnp.stack([upper, middle, lower])
    return payload


def joined(merged, received, is_right):
    upper, upper_right, lower_left, lower = quarters(merged)
    partner_upper = received[0]
    partner_middle = received[1]
    partner_lower = received[2]
    left_upper = jnp.where(is_right, partner_upper, upper)
    left_lower_left = jnp.where(is_right, partner_middle, lower_left)
    left_lower = jnp.where(is_right, partner_lower, lower)
    right_upper = jnp.where(is_right, upper, partner_upper)
    right_upper_right = jnp.where(is_right, upper_right, partner_middle)
    right_lower = jnp.where(is_right, lower, partner_lower)
    return merge_blocks(
        left_upper, left_lower_left, left_lower, right_upper, right_upper_right, right_lower
    )


def local_columns(classes, across_coeff, along_coeff):
    across = lookup(classes, across_coeff)
    along = lookup(classes, along_coeff)
    own_map = piece_map(across, along)
    col_levels = lax.axis_size("col").bit_length() - 1
    slab_levels = lax.axis_size("slab").bit_length() - 1
    merged = own_map
    for height in range(col_levels):
        is_right = lax.axis_index("col") >> height & 1 == 1
        received = swapped(level_payload(merged, is_right), "col", height)
        merged = joined(merged, received, is_right)
    for height in range(slab_levels):
        is_right = lax.axis_index("slab") >> height & 1 == 1
        received = swapped(level_payload(merged, is_right), "slab", height)
        merged = joined(merged, received, is_right)
    share_rows = merged.shape[0] // lax.axis_size(("slab", "col"))
    root_rows = lax.dynamic_slice_in_dim(
        merged, lax.axis_index(("slab", "col")) * share_rows, share_rows, 0
    )
    return (own_map, root_rows)


def piece_kernel(size, rows, vec_ref, cols_ref, o_ref, coef):
    levels = size.bit_length() - 1
    i = pl.program_id(0)

    def back(x, s):
        return pltpu.roll(x, s, 1)

    def fore(x, s):
        return pltpu.roll(x, size - s, 1)

    @pl.when(i == 0)
    def _():
        def wide(k):
            return jnp.broadcast_to(vec_ref[k : k + 1, :], (8, size))

        a0, a1, al0, al1 = wide(0), wide(1), wide(2), wide(3)
        sh1 = back(al1, 1)
        diag = a0 + a1 + al1 + sh1
        inv = 1.0 / diag
        coef[0] = inv
        lo = -sh1 * inv
        hi = -al1 * inv
        for level in range(levels - 1):
            s = 1 << level
            fix = 1.0 / (1.0 - lo * back(hi, s) - hi * fore(lo, s))
            coef[3 * level + 1] = -lo
            coef[3 * level + 2] = -hi
            coef[3 * level + 3] = fix
            lo, hi = -lo * back(lo, s) * fix, -hi * fore(hi, s) * fix
        g = lo + hi
        h = back(g, size // 2)
        coef[3 * levels - 2] = -g
        coef[3 * levels - 1] = 1.0 / (1.0 - g * h)

    def co(k):
        return coef[k, 0:1, :]

    row = lax.broadcasted_iota(jnp.int32, (rows, size), 0) + i * rows
    col = lax.broadcasted_iota(jnp.int32, (rows, size), 1)
    x = jnp.where(row == col, co(0), 0.0)
    for level in range(levels - 1):
        s = 1 << level
        x = (x + co(3 * level + 1) * back(x, s) + co(3 * level + 2) * fore(x, s)) * co(3 * level + 3)
    x = (x + co(3 * levels - 2) * back(x, size // 2)) * co(3 * levels - 1)
    a0, a1, al0 = vec_ref[0:1, :], vec_ref[1:2, :], vec_ref[2:3, :]
    sh0 = jnp.broadcast_to(vec_ref[4:5, :], (1, size))
    r0, r1 = cols_ref[:, 0:1], cols_ref[:, 1:2]
    vert = jnp.where(row == col, al0 + sh0 + a0, 0.0)
    vert = vert - jnp.where(row == jnp.where(col == size - 1, 0, col + 1), al0, 0.0)
    vert = vert - jnp.where(col == jnp.where(row == size - 1, 0, row + 1), sh0, 0.0)
    x0, x1 = x * a0, x * a1
    o_ref[0, :, :size] = vert - r0 * x0
    o_ref[0, :, size:] = -(r0 * x1)
    o_ref[1, :, :size] = -(r1 * x0)
    o_ref[1, :, size:] = jnp.where(row == col, a1, 0.0) - r1 * x1


def piece_map(across, along):
    size = across.shape[1]
    rows = 32
    vecs = jnp.concatenate([across, along, jnp.roll(along, 1, axis=1), along], axis=0)
    out = pl.pallas_call(
        functools.partial(piece_kernel, size, rows),
        grid=(size // rows,),
        out_shape=jax.ShapeDtypeStruct((2, size, 2 * size), jnp.float32),
        in_specs=[
            pl.BlockSpec((8, size), lambda i: (0, 0)),
            pl.BlockSpec((rows, 2), lambda i: (i, 0)),
        ],
        out_specs=pl.BlockSpec((2, rows, 2 * size), lambda i: (0, i, 0)),
        scratch_shapes=[pltpu.VMEM((3 * (size.bit_length() - 1), 8, size), jnp.float32)],
    )(vecs, across.T)
    return out.reshape(2 * size, 2 * size)


def gather_kernel(slabs, cols, x_ref, o_ref, send, recv, pass_send, pass_recv, own):
    half = cols // 2
    pairs = slabs * half
    slab, col = lax.axis_index("slab"), lax.axis_index("col")
    pair, odd = slab * half + col // 2, lax.rem(col, 2)
    me = slab * cols + col

    def place(q, side):
        return {"slab": q // half, "col": lax.rem(q, half) * 2 + side}

    def index(q, side):
        return q * 2 + side

    def to(step):
        return lax.rem(pair + step, pairs)

    def copy(src, at, sems, step, device):
        return pltpu.make_async_remote_copy(
            src_ref=src,
            dst_ref=o_ref.at[at],
            send_sem=sems[0].at[step],
            recv_sem=sems[1].at[step],
            device_id=device,
            device_id_type=pl.DeviceIdType.MESH,
        )

    barrier = pltpu.get_barrier_semaphore()
    sibling = place(pair, 1 - odd)
    for step in range(1, pairs):
        pl.semaphore_signal(
            barrier, inc=1, device_id=place(to(step), odd), device_id_type=pl.DeviceIdType.MESH
        )
    pl.semaphore_signal(barrier, inc=1, device_id=sibling, device_id_type=pl.DeviceIdType.MESH)
    pl.semaphore_wait(barrier, pairs)

    local_copy = pltpu.make_async_copy(x_ref, o_ref.at[me], own)
    local_copy.start()
    out = [copy(x_ref, me, (send, recv), step, place(to(step), odd)) for step in range(1, pairs)]
    for c in out:
        c.start()
    passed = [copy(x_ref, me, (pass_send, pass_recv), 0, sibling)]
    passed[0].start()
    for step in range(1, pairs):
        at = index(to(pairs - step), odd)
        copy(x_ref, at, (send, recv), step, sibling).wait_recv()
        c = copy(o_ref.at[at], at, (pass_send, pass_recv), step, sibling)
        c.start()
        passed.append(c)
    for step in range(pairs):
        at = index(to(pairs - step), 1 - odd)
        copy(x_ref, at, (pass_send, pass_recv), step, sibling).wait_recv()
    for c in out + passed:
        c.wait_send()
    local_copy.wait()


def gathered(block, number):
    slabs, cols = lax.axis_size("slab"), lax.axis_size("col")
    if cols % 2:
        return lax.all_gather(block, AXES, axis=0)
    pairs = slabs * cols // 2
    return pl.pallas_call(
        functools.partial(gather_kernel, slabs, cols),
        out_shape=jax.ShapeDtypeStruct((slabs * cols,) + block.shape, block.dtype),
        in_specs=[pl.BlockSpec(memory_space=pltpu.VMEM)],
        out_specs=pl.BlockSpec(memory_space=pltpu.VMEM),
        scratch_shapes=[pltpu.SemaphoreType.DMA((pairs,))] * 4 + [pltpu.SemaphoreType.DMA],
        compiler_params=pltpu.CompilerParams(collective_id=number, has_side_effects=True),
    )(block)


LANES = 128
SUBS = 8


def spread(x):
    return jnp.broadcast_to(x, (SUBS, LANES))


def tree(terms):
    while len(terms) > 1:
        terms = [sum(terms[k : k + 2][1:], terms[k]) for k in range(0, len(terms), 2)]
    return terms[0]


def minus_inverse(v):
    size = len(v)
    v = [list(row) for row in v]
    for k in range(0, size, 2):
        p, q, r = v[k][k], v[k][k + 1], v[k + 1][k + 1]
        inv = 1.0 / (p * r - q * q)
        others = [i for i in range(size) if i not in (k, k + 1)]
        c = {i: (v[min(i, k)][max(i, k)], v[min(i, k + 1)][max(i, k + 1)]) for i in others}
        s = {}
        for i in others:
            x, y = c[i]
            s[i] = ((r * x - q * y) * inv, (p * y - q * x) * inv)
        for i in others:
            for j in others:
                if i <= j:
                    v[i][j] = v[i][j] - (s[i][0] * c[j][0] + s[i][1] * c[j][1])
        for i in others:
            sign = 1.0 if i < k else -1.0
            for d in range(2):
                v[min(i, k + d)][max(i, k + d)] = s[i][d]
        v[k][k], v[k][k + 1], v[k + 1][k + 1] = -(r * inv), q * inv, -(p * inv)
    return [[v[min(i, j)][max(i, j)] for j in range(size)] for i in range(size)]


def eliminate(g, n, vals, invs):
    count, tiles = len(g), n // SUBS
    half_tiles = tiles // 2 if count > 1 else tiles
    for p in range(tiles):
        at = p * SUBS
        mine = range(0, half_tiles) if p < half_tiles else range(half_tiles, tiles)
        for j in range(SUBS):
            for b in range(count):
                vals[j, b * SUBS : (b + 1) * SUBS] = spread(g[b][p][0][:, at + j : at + j + 1])
        v = [
            [vals[j, pl.ds(i, SUBS, stride=SUBS)] if i <= j else None for j in range(SUBS)]
            for i in range(SUBS)
        ]
        w = minus_inverse(v)
        for j in range(SUBS):
            for i in range(SUBS):
                invs[j, i * SUBS : (i + 1) * SUBS] = w[i][j]
        for b in range(count):
            m = [invs[j, pl.ds(b, SUBS, stride=SUBS)] for j in range(SUBS)]
            s = [
                tree([m[j] * spread(half[j : j + 1]) for j in range(SUBS)]) for half in g[b][p]
            ]
            rows = [i for i in mine if i != p]
            old = {i: g[b][i][0] for i in rows}
            for j in range(SUBS):
                wide = [spread(half[j : j + 1]) for half in s]
                for i in rows:
                    c = spread(old[i][:, at + j : at + j + 1])
                    g[b][i] = [half + c * wide[h] for h, half in enumerate(g[b][i])]
            g[b][p] = [-half for half in s]
        if half_tiles < tiles and p + 1 in (half_tiles, tiles):
            others = [i for i in range(tiles) if i not in mine]
            zero = jnp.zeros((len(others) * SUBS, 2 * LANES), jnp.float32)
            for b in range(count):
                done = jnp.concatenate([jnp.concatenate(g[b][i], axis=1) for i in mine], axis=0)
                done = jnp.concatenate([done, zero] if p < half_tiles else [zero, done], axis=0)
                rest = jnp.concatenate([g[b][i][0] for i in others], axis=0)[:, :n]
                u = contract(rest, done, 1)
                for q, i in enumerate(others):
                    g[b][i] = [
                        half - u[q * SUBS : (q + 1) * SUBS, h * LANES : (h + 1) * LANES]
                        for h, half in enumerate(g[b][i])
                    ]
    return g


def halves(x):
    return [x[:, :LANES], x[:, LANES:]]


def parts(x):
    high = x.astype(jnp.bfloat16)
    return high, (x - high.astype(jnp.float32)).astype(jnp.bfloat16)


def contract(a, b, dim):
    def dot(x, y):
        return lax.dot_general(
            x, y, (((dim,), (0,)), ((), ())), preferred_element_type=jnp.float32
        )

    (ah, al), (bh, bl) = parts(a), parts(b)
    return dot(ah, bh) + (dot(ah, bl) + dot(al, bh))


def product(a, b):
    return contract(a, b, 1)


def product_t(a, b):
    return contract(a, b, 0)


def merge_group(src, dst, keep, lefts, n, vals, invs):
    rows = src.shape[1]
    g = [
        [
            halves(src[2 * l, n + k : n + k + SUBS] + src[2 * l + 1, k : k + SUBS])
            for k in range(0, n, SUBS)
        ]
        for l in lefts
    ]
    g = eliminate(g, n, vals, invs)
    lane = lax.broadcasted_iota(jnp.int32, (1, LANES), 1)
    for l, x in zip(lefts, g):
        z = jnp.concatenate([jnp.concatenate(h, axis=1) for h in x], axis=0)
        if keep is not None:
            keep[l] = z
        top, low = src[2 * l, 0:n], src[2 * l + 1, n : 2 * n]
        base = [top, low]
        if rows > 2 * n:
            base.append(src[2 * l, 2 * n :] + src[2 * l + 1, 2 * n :])
        base = jnp.concatenate(base, axis=0)
        new = base - product(base[:, :n], z)
        v0, v1 = halves(new)
        if dst is None:
            return v0, v1
        odd = l % 2
        if isinstance(odd, int):
            if odd:
                v0, v1 = jnp.where(lane < n, pltpu.roll(v0, n, 1), 0.0), v1
            else:
                v0, v1 = jnp.where(lane < n, v1, v0), jnp.where(lane < n, 0.0, v1)
        dst[l, :, :LANES] = v0
        dst[l, :, LANES:] = v1


def local_kernel(n, height, cls_ref, ac_ref, al_ref, o_ref, first, second, vals, invs):
    k = 2 * height
    lane = lax.broadcasted_iota(jnp.int32, (1, LANES), 1)
    cls = cls_ref[...]
    across = jnp.zeros(cls.shape, jnp.float32)
    along = jnp.zeros(cls.shape, jnp.float32)
    for level in range(ac_ref.shape[0]):
        across = jnp.where(cls == level, ac_ref[level], across)
        along = jnp.where(cls == level, al_ref[level], along)
    inner = (lane > 0) & (lane < n)
    link = jnp.where(inner, along, 0.0)
    before = pltpu.roll(across, 1, 1)
    off = jnp.where(inner, across, 0.0)
    i = lax.broadcasted_iota(jnp.int32, (n, LANES), 0)
    j = lax.broadcasted_iota(jnp.int32, (n, LANES), 1)
    kr = lax.broadcasted_iota(jnp.int32, (k, LANES), 0)
    kl = lax.broadcasted_iota(jnp.int32, (k, LANES), 1)
    zero = jnp.zeros((n, LANES), jnp.float32)
    for h in range(height):
        a, prev = across[h + 1 : h + 2], link[h : h + 1]
        diag = jnp.where(inner, before[h + 1 : h + 2] + a + along[h : h + 1] + along[h + 1 : h + 2], 1.0)
        right = off[h + 1 : h + 2]
        left = jnp.where(lane > 0, pltpu.roll(right, 1, 1), 0.0)
        bb = jnp.where(i == j, diag, 0.0) - jnp.where(j == i + 1, left, 0.0) - jnp.where(i == j + 1, right, 0.0)
        bb = jnp.where(j < n, bb, 0.0)
        tb = -jnp.where((i == j) & (j < n), prev, 0.0)
        a0, a1 = a[:, 0:1], a[:, n - 1 : n]
        fb = -jnp.where((i == 1) & (j == n + h), a0, 0.0) - jnp.where((i == n - 1) & (j == n + height + h), a1, 0.0)
        ft = -jnp.where((kr == h) & (kl == 1), a0, 0.0) - jnp.where((kr == height + h) & (kl == n - 1), a1, 0.0)
        if h % 2:
            first[h, 0:n, :LANES] = zero
            first[h, 0:n, LANES:] = tb
            first[h, n : 2 * n, :LANES] = tb
            first[h, n : 2 * n, LANES:] = bb + fb
            first[h, 2 * n :, :LANES] = jnp.zeros((k, LANES), jnp.float32)
            first[h, 2 * n :, LANES:] = ft
        else:
            first[h, 0:n, :LANES] = tb
            first[h, 0:n, LANES:] = zero
            first[h, n : 2 * n, :LANES] = bb + pltpu.roll(tb, n, 1)
            first[h, n : 2 * n, LANES:] = fb
            first[h, 2 * n :, :LANES] = ft
            first[h, 2 * n :, LANES:] = jnp.zeros((k, LANES), jnp.float32)
    count, src, dst = height // 2, first, second
    while count > 1:
        merge_group(src, dst, None, list(range(count)), n, vals, invs)
        src, dst, count = dst, src, count // 2
    v0, v1 = merge_group(src, None, None, [0], n, vals, invs)
    top = jnp.where(lane < n, pltpu.roll(v0[:n], n, 1), pltpu.roll(v1[:n], n, 1))
    o_ref[0:n] = top
    o_ref[n : 2 * n] = jnp.where(lane < n + k, v1[n : 2 * n], pltpu.roll(v1[:n], k, 1))
    kk = v1[2 * n :]
    packed = None
    for q in range(k // SUBS):
        piece = pltpu.roll(kk[q * SUBS : (q + 1) * SUBS], (q * k - n) % LANES, 1)
        packed = piece if q == 0 else jnp.where(lane // k == q, piece, packed)
    o_ref[2 * n :] = packed


def local_strip(cls, across_coeff, along_coeff, n, height):
    k = 2 * height
    rows = 2 * n + k
    return pl.pallas_call(
        functools.partial(local_kernel, n, height),
        out_shape=jax.ShapeDtypeStruct((2 * n + SUBS, LANES), jnp.float32),
        in_specs=[
            pl.BlockSpec(memory_space=pltpu.VMEM),
            pl.BlockSpec(memory_space=pltpu.SMEM),
            pl.BlockSpec(memory_space=pltpu.SMEM),
        ],
        out_specs=pl.BlockSpec(memory_space=pltpu.VMEM),
        scratch_shapes=[
            pltpu.VMEM((height, rows, 2 * LANES), jnp.float32),
            pltpu.VMEM((height // 2, rows, 2 * LANES), jnp.float32),
            pltpu.VMEM((SUBS, SUBS * SUBS, LANES), jnp.float32),
            pltpu.VMEM((SUBS, SUBS * SUBS, LANES), jnp.float32),
        ],
    )(cls, across_coeff, along_coeff)


def ring_kernel(n, height, where_ref, x_ref, o_ref, first, kept, xs, vals, invs):
    strips = x_ref.shape[0]
    k = 2 * height
    lane = lax.broadcasted_iota(jnp.int32, (1, LANES), 1)
    s0, side = where_ref[0], where_ref[1]
    left_half = lane < n

    @pl.loop(0, strips // 2)
    def _(q):
        a0, a1 = x_ref[2 * q, 0:n], x_ref[2 * q, n : 2 * n]
        b0, b1 = x_ref[2 * q + 1, 0:n], x_ref[2 * q + 1, n : 2 * n]
        both = jnp.where(left_half, pltpu.roll(a0, n, 1), b0)
        both = jnp.concatenate([both, jnp.zeros((n, LANES), jnp.float32)], axis=0).T
        zero = jnp.zeros((n, LANES), jnp.float32)
        e, f = 2 * q, 2 * q + 1
        first[e, 0:n, :LANES] = pltpu.roll(a0, n, 1)
        first[e, 0:n, LANES:] = zero
        first[e, n : 2 * n, :LANES] = jnp.where(left_half, a1, pltpu.roll(both[:n], n, 1))
        first[e, n : 2 * n, LANES:] = zero
        first[f, 0:n, :LANES] = jnp.where(left_half, b0, 0.0)
        first[f, 0:n, LANES:] = jnp.where(left_half, pltpu.roll(b0, n, 1), 0.0)
        first[f, n : 2 * n, :LANES] = both[n:]
        first[f, n : 2 * n, LANES:] = jnp.where(left_half, b1, 0.0)

    for a in range(2):
        s = s0 + a
        low = x_ref[s, n : 2 * n]
        mine = (lane >= n + a * height) & (lane < n + (a + 1) * height)
        shift = (a - side) * height
        fb = jnp.where(mine, pltpu.roll(low, lax.rem(shift + LANES, LANES), 1), 0.0)
        ft = jnp.where(mine, pltpu.roll(low, lax.rem(shift - k + LANES, LANES), 1), 0.0)
        first[s, 0:n, LANES:] += ft
        first[s, n : 2 * n, LANES:] += fb

    merges, bases, count = 0, [], strips // 2
    while count:
        bases.append((merges, count))
        merges, count = merges + count, count // 2
    grouped = sum(c for _, c in bases if c >= SUBS)

    @pl.loop(0, grouped // SUBS)
    def _(g):
        at = g * SUBS
        merge_group(
            first.at[pl.ds(2 * at, 2 * SUBS)], first.at[pl.ds(strips + at, SUBS)],
            kept.at[pl.ds(at, SUBS)], list(range(SUBS)), n, vals, invs,
        )

    for base, count in bases:
        if count < SUBS:
            src, keep = first.at[pl.ds(2 * base, 2 * count)], kept.at[pl.ds(base, count)]
            dst = first.at[pl.ds(strips + base, count)] if count > 1 else None
            out = merge_group(src, dst, keep, list(range(count)), n, vals, invs)
    v0, v1 = out
    d = pltpu.roll(v0[:n], n, 1) + v1[:n] + pltpu.roll(v0[n:], n, 1) + v1[n:]
    f = v1[:n] + v1[n:]
    d = jnp.where(left_half, d, 0.0)
    g = [[[d[r : r + SUBS], f[r : r + SUBS]] for r in range(0, n, SUBS)]]
    g = eliminate(g, n, vals, invs)
    x = jnp.concatenate([h[1] for h in g[0]], axis=0)
    xs[strips - 1] = x
    step = strips // 2
    for base, count in reversed(bases):
        for l in range(count):
            at = (2 * l + 1) * step - 1
            t_at, b_at = (at - step) % strips, (at + step) % strips
            z = kept[base + l]
            both = jnp.concatenate([xs[t_at], xs[b_at]], axis=0)
            zz = jnp.where(left_half, pltpu.roll(z[:, :LANES], n, 1), pltpu.roll(z[:, LANES:], n, 1))
            xs[at] = z[:, LANES:] - product(zz, both)
        step //= 2

    outs = [[None] * (strips * height // LANES) for _ in range(2)]
    per = LANES // height
    for s in range(strips):
        xx = jnp.where(left_half, pltpu.roll(xs[s], n, 1), xs[(s - 1) % strips])
        r = product_t(xx, x_ref[s, n : 2 * n])
        r = r[:k] + pltpu.roll(r[n : n + k], LANES - k, 1)
        block, spot = s // per, s % per
        for side_of in range(2):
            piece = pltpu.roll(r, (spot * height - n - side_of * height) % LANES, 1)
            old = outs[side_of][block]
            outs[side_of][block] = -piece if old is None else jnp.where(lane // height == spot, -piece, old)
    o_ref[...] = jnp.concatenate(outs[0] + outs[1], axis=1)
    for a in range(2):
        s = s0 + a
        kk = x_ref[s, 2 * n : 2 * n + SUBS]
        spot, block = lax.rem(s, per), s // per
        for h in range(height // SUBS):
            q = side * (height // SUBS) + h
            for side_of in range(2):
                shift = spot * height - q * k - side_of * height + 4 * LANES
                piece = pltpu.roll(kk, lax.rem(shift, LANES), 1)
                at = pl.multiple_of((side_of * (strips // per) + block) * LANES, LANES)
                rows = pl.ds(a * height + h * SUBS, SUBS)
                o_ref[rows, pl.ds(at, LANES)] += jnp.where(lane // height == spot, piece, 0.0)


def ring_rows(where, wide, n, height):
    strips, k = wide.shape[0], 2 * height
    return pl.pallas_call(
        functools.partial(ring_kernel, n, height),
        out_shape=jax.ShapeDtypeStruct((k, k * strips), jnp.float32),
        in_specs=[
            pl.BlockSpec(memory_space=pltpu.SMEM),
            pl.BlockSpec(memory_space=pltpu.VMEM),
        ],
        out_specs=pl.BlockSpec(memory_space=pltpu.VMEM),
        scratch_shapes=[
            pltpu.VMEM((2 * strips, 2 * n, 2 * LANES), jnp.float32),
            pltpu.VMEM((strips, n, 2 * LANES), jnp.float32),
            pltpu.VMEM((strips, n, LANES), jnp.float32),
            pltpu.VMEM((SUBS, SUBS * SUBS, LANES), jnp.float32),
            pltpu.VMEM((SUBS, SUBS * SUBS, LANES), jnp.float32),
        ],
    )(where, wide)


def relay_kernel(slabs, cols, x_ref, o_ref, send, recv, own):
    sides = 2
    depth, height = slabs // sides, cols // 2
    slab, col = lax.axis_index("slab"), lax.axis_index("col")
    z, y, x, core = slab // sides, lax.rem(slab, sides), col // 2, lax.rem(col, 2)

    def place(x, y, z, core):
        return {"slab": z * sides + y, "col": x * 2 + core}

    def index(x, y, z, core):
        return (z * sides + y) * cols + x * 2 + core

    def along(step):
        return lax.rem(z + step, depth)

    across_x, across_y, sibling = (1 - x, y, z, core), (x, 1 - y, z, core), (x, y, z, 1 - core)
    lines = [(x, y, along(step), core) for step in range(1, depth)]
    barrier = pltpu.get_barrier_semaphore()
    for target in lines + [across_x, across_y, sibling]:
        pl.semaphore_signal(
            barrier, inc=1, device_id=place(*target), device_id_type=pl.DeviceIdType.MESH
        )
    pl.semaphore_wait(barrier, depth + 2)

    started = []

    def copy(src, at, slot, target):
        return pltpu.make_async_remote_copy(
            src_ref=src, dst_ref=o_ref.at[at], send_sem=send.at[slot], recv_sem=recv.at[at],
            device_id=place(*target), device_id_type=pl.DeviceIdType.MESH,
        )

    def forward(src, at, targets):
        for target in targets:
            c = copy(src, at, len(started), target)
            c.start()
            started.append(c)

    def arrived(at):
        copy(x_ref, at, 0, sibling).wait_recv()

    def relay(at, targets):
        arrived(at)
        forward(o_ref.at[at], at, targets)

    me = index(x, y, z, core)
    local_copy = pltpu.make_async_copy(x_ref, o_ref.at[me], own)
    local_copy.start()
    forward(x_ref, me, [across_x, across_y] + lines + [sibling])
    half = max(depth // 2, 1)
    order = [0]
    for d in range(1, depth // 2 + 1):
        order += sorted({d, depth - d})
    for step in order:
        at = along(step)
        if step:
            relay(index(x, y, at, core), [across_x, across_y, sibling])
        first = step < half
        relay(index(1 - x, y, at, core), [across_y, sibling] if first else [sibling])
        relay(index(x, 1 - y, at, core), [sibling] if first else [across_x, sibling])
    for step in order:
        relay(index(1 - x, 1 - y, along(step), core), [sibling])
    for step in order:
        for other in ((x, y), (1 - x, y), (x, 1 - y), (1 - x, 1 - y)):
            arrived(index(*other, along(step), 1 - core))
    for c in started:
        c.wait_send()
    local_copy.wait()


def relayed(block, number):
    slabs, cols = lax.axis_size("slab"), lax.axis_size("col")
    if cols != 4 or slabs % 2:
        return gathered(block, number)
    return pl.pallas_call(
        functools.partial(relay_kernel, slabs, cols),
        out_shape=jax.ShapeDtypeStruct((slabs * cols,) + block.shape, block.dtype),
        in_specs=[pl.BlockSpec(memory_space=pltpu.VMEM)],
        out_specs=pl.BlockSpec(memory_space=pltpu.VMEM),
        scratch_shapes=[
            pltpu.SemaphoreType.DMA((2 * slabs * cols,)),
            pltpu.SemaphoreType.DMA((slabs * cols,)),
            pltpu.SemaphoreType.DMA,
        ],
        compiler_params=pltpu.CompilerParams(collective_id=number, has_side_effects=True),
    )(block)


def local_rows(classes, across_coeff, along_coeff):
    own_across = lookup(classes, across_coeff)
    own_along = lookup(classes, along_coeff)
    devices = lax.axis_size(AXES)
    me = lax.axis_index(AXES)
    size = classes.shape[1]
    cols = classes.shape[0] * devices
    height = size // devices
    everyone = gathered(classes, 0).reshape(cols, size)
    own_map = piece_map(own_across, own_along)
    padded = jnp.concatenate([everyone[:, size - 1 :], everyone], axis=1)
    mine = lax.dynamic_slice_in_dim(padded, me * height, height + 1, 1).T
    mine = jnp.pad(mine, ((0, -(height + 1) % SUBS), (0, LANES - cols)))
    wide = relayed(local_strip(mine, across_coeff, along_coeff, cols, height), 1)
    share = 2 * size // devices
    start = me * share
    side = start // size
    where = jnp.stack([(start - side * size) // height, side]).astype(jnp.int32)
    rows = ring_rows(where, wide, cols, height)

    first_ac = lookup(everyone[:1], across_coeff)
    last_ac = lookup(everyone[cols - 1 :], across_coeff)
    al = lookup(everyone[:1], along_coeff)
    sh = jnp.roll(al, 1, axis=1)
    zero = jnp.zeros_like(al)
    on = jnp.concatenate([first_ac + al + sh, last_ac], axis=1)
    below = jnp.concatenate([al, zero], axis=1)
    above = jnp.concatenate([sh, zero], axis=1)
    row = lax.broadcasted_iota(jnp.int32, (share, 2 * size), 0) + start
    col = lax.broadcasted_iota(jnp.int32, (share, 2 * size), 1)
    rows = rows + jnp.where(row == col, on, 0.0)
    rows = rows - jnp.where((row == (col + 1) % size) & (row < size) & (col < size), below, 0.0)
    rows = rows - jnp.where((col == (row + 1) % size) & (row < size) & (col < size), above, 0.0)
    return own_map, rows


def local(classes, across_coeff, along_coeff):
    devices = lax.axis_size(AXES)
    cols = classes.shape[0] * devices
    height = classes.shape[1] // devices
    if 2 * cols == LANES and 4 * height == cols:
        return local_rows(classes, across_coeff, along_coeff)
    return local_columns(classes, across_coeff, along_coeff)


def solution(mesh):
    placed = (P(("slab", "col"), None), P(), P())
    return jax.shard_map(
        local,
        mesh=mesh,
        in_specs=placed,
        out_specs=(P(("slab", "col"), None), P(("slab", "col"), None)),
        check_vma=False,
    )
```
